32 devices in a mesh: case: 2 (over x), axial: 16 (over z, y, core).
Axes of the slice: x: 2, y: 2, z: 4, core: 2. Of those that a mesh axis runs over, the one named last changes fastest.
Arguments:
- forced_pairs: int32 [32, 2], P('case'), parts along dimension 0, may hold values from 0 to 32, as said below
- cell_type: int32 [768, 512], P(('case', 'axial')), parts along dimension 0, may hold values from 0 to 2, as said below
- mean_density: float32 [768, 512], P(('case', 'axial')), parts along dimension 0, may hold values from 0.7 to 1.3
- mean_velocity: float32 [6, 384, 512], P('case', 'axial'), parts along dimension 0, may hold values from -3 to 3
- mean_pressure: float32 [768, 512], P(('case', 'axial')), parts along dimension 0, may hold values from 0.5 to 0.9
- eddy_visc: float32 [768, 512], P(('case', 'axial')), parts along dimension 0, may hold values from 0.02 to 0.3
- forcing: float32 [4, 5, 384, 512], P('case', None, 'axial'), parts along dimension 0, may hold values from -6 to 6
Outputs:
- responses: float32 [32, 2, 5, 384, 512], P('case', None, None, 'axial'), parts along dimension 0
- correction: float32 [4, 384, 512], P('case', 'axial'), parts along dimension 0
The draws below stay inside these ranges and needn't reach their ends.
There are 2 independent parts, one for each index of `case`. The reference program is written for one: setup_inputs(seed, part) draws one part's arguments, and reference() takes and returns one part's arrays. A program takes and returns all parts, laid end to end along the dimension named above; each array names one. Nothing has to cross between parts.
Inputs may be any that keep to these rules, and one draw needn't show every extreme that they name: `forced_pairs`: column 0 is a frequency index of 1 to 32, column 1 an azimuthal wavenumber of 0 to 4. `cell_type`: 0 marks a fluid cell, 1 a sponge cell, 2 a nozzle wall cell.
All inputs are finite; a program needn't handle non-finite values.
Results may differ from the reference program's by a relative error of at most 0.00002.
Values sent between devices are 32-bit elements; how exact they have to be, the bound alone decides.
A program may use at most 128 MiB of HBM per device.

```python
import math
import jax
import jax.numpy as jnp
from jax import lax

NR = 512
PAIRS = 16
SWEEPS = 2
NXT = 384


def draw_forced_pairs(key, part):
    key_first, key_second = jax.random.split(key)
    column_one = jax.random.randint(key_first, (PAIRS, 1), 1, 33)
    column_two = jax.random.randint(key_second, (PAIRS, 1), 0, 5)
    return jnp.concatenate([column_one, column_two], axis=1).astype(jnp.int32)


def draw_cell_type(key, part):
    key_first, key_second = jax.random.split(key)
    thickness = jax.random.randint(key_first, (NXT, 1), NR // 16, NR // 8 + 1)
    lip_row = jax.random.randint(key_second, (), NR // 8, NR // 4)
    axial_index = jnp.arange(NXT)[:, None]
    radial_index = jnp.arange(NR)[None, :]
    sponge = (radial_index >= NR - thickness) | (axial_index >= NXT - NXT // 8)
    wall = (axial_index < NXT // 16) & (jnp.abs(radial_index - lip_row) <= 1)
    return jnp.where(wall, 2, jnp.where(sponge, 1, 0)).astype(jnp.int32)


def steps_of(key, extent, cuts, smallest, high):
    loudness = 1.0
    for axis_at, blocks in cuts:
        steps = jax.random.uniform(jax.random.fold_in(jax.random.fold_in(key, 6), axis_at), (blocks,), jnp.float32, smallest / len(cuts), high / len(cuts))
        loudness = loudness * jnp.repeat(jnp.exp(steps), extent[axis_at] // blocks).reshape((-1,) + (1,) * (len(extent) - 1 - axis_at))
    return loudness


def noise(stream_key, shape, deviation, limit, pieces=(), kind=jnp.bfloat16):
    values = jax.random.normal(stream_key, shape, jnp.float32) * deviation
    if len(pieces) > 0:
        values = steps_of(stream_key, shape, pieces, -0.22, 0.18) * values
    return jnp.clip(values, min=-limit, max=limit).astype(kind)


def setup_inputs(seed: int = 0, part: int = 0) -> dict:
    key_of = jax.random.split(jax.random.key(seed), 8)
    part_keys = jax.random.split(jax.random.fold_in(key_of[7], part), 8)
    return {
        "forced_pairs": draw_forced_pairs(jax.random.fold_in(jax.random.fold_in(key_of[7], part), 71), part),
        "cell_type": draw_cell_type(jax.random.fold_in(jax.random.fold_in(key_of[7], part), 71), part),
        "mean_density": jnp.clip(0.7 + 0.59999996 * jax.random.uniform(part_keys[2], (NXT, NR), jnp.float32) ** steps_of(part_keys[2], (NXT, NR), ((0, 16),), -0.2, 0.2), 0.7, 1.3),
        "mean_velocity": noise(part_keys[3], (3, NXT, NR), 0.5, 3.0, ((1, 16),), jnp.float32),
        "mean_pressure": jnp.clip(0.5 + 0.39999998 * jax.random.uniform(part_keys[4], (NXT, NR), jnp.float32) ** steps_of(part_keys[4], (NXT, NR), ((0, 16),), -0.2, 0.2), 0.5, 0.9),
        "eddy_visc": jnp.clip(jnp.exp(math.log(0.3) - 2.7080503 * jax.random.uniform(part_keys[5], (NXT, NR), jnp.float32) ** steps_of(part_keys[5], (NXT, NR), ((0, 16),), -0.2, 0.2)), 0.02, 0.3),
        "forcing": noise(part_keys[6], (2, 5, NXT, NR), 1.0, 6.0, ((2, 16),), jnp.float32),
    }


heat_ratio = 1.4
pseudo_step = 0.1

def axial_diff(source):
    return (source[..., :-4, :] - 8.0 * source[..., 1:-3, :] + 8.0 * source[..., 3:-1, :] - source[..., 4:, :]) / 12.0

def axial_second(source):
    return (-source[..., :-4, :] + 16.0 * source[..., 1:-3, :] - 30.0 * source[..., 2:-2, :] + 16.0 * source[..., 3:-1, :] - source[..., 4:, :]) / 12.0

def radial_pad(source):
    widths = [(0, 0)] * (source.ndim - 1) + [(1, 1)]
    return jnp.pad(source, widths)

def radial_diff(source):
    padded = radial_pad(source)
    return 0.5 * (padded[..., 2:] - padded[..., :-2])

def radial_second(source):
    padded = radial_pad(source)
    return padded[..., 2:] - 2.0 * source + padded[..., :-2]

def times_unit(real_imag, part_idx):
    if part_idx == 0:
        return -real_imag[1]
    return real_imag[0]

def coefficients(mean_ext, viscosity, damping, inverse_r):
    center = mean_ext[:, 2:-2, :]
    return (center, axial_diff(mean_ext), radial_diff(center), viscosity, damping, inverse_r)

def sweep(padded, coeffs, wavenumber, frequency, drive):
    center, axial_grad, radial_grad, viscosity, damping, inverse_r = coeffs
    density, axial_vel, radial_vel, swirl_vel, pressure = (center[0], center[1], center[2], center[3], center[4])
    inv_density = 1.0 / density
    azimuth = wavenumber * inverse_r
    interior = [[padded[..., part_idx, comp_idx, 2:-2, :] for comp_idx in range(5)] for part_idx in range(2)]
    outputs = []
    for part_idx in range(2):
        current = interior[part_idx]
        d_axial = [axial_diff(padded[..., part_idx, comp_idx, :, :]) for comp_idx in range(5)]
        d_radial = [radial_diff(current[comp_idx]) for comp_idx in range(5)]
        turned = [times_unit((interior[0][comp_idx], interior[1][comp_idx]), part_idx) for comp_idx in range(5)]
        convect = [axial_vel * d_axial[comp_idx] + radial_vel * d_radial[comp_idx] + swirl_vel * azimuth * turned[comp_idx] for comp_idx in range(5)]
        divergence = d_axial[1] + d_radial[2] + current[2] * inverse_r + azimuth * turned[3]
        viscous = [viscosity * (axial_second(padded[..., part_idx, comp_idx, :, :]) + radial_second(current[comp_idx]) + d_radial[comp_idx] * inverse_r - azimuth * azimuth * current[comp_idx]) for comp_idx in range(5)]
        tendency = [-convect[0] - density * divergence - current[1] * axial_grad[0] - current[2] * radial_grad[0], -convect[1] - current[1] * axial_grad[1] - current[2] * radial_grad[1] - inv_density * d_axial[4] + viscous[1], -convect[2] - current[1] * axial_grad[2] - current[2] * radial_grad[2] + 2.0 * swirl_vel * inverse_r * current[3] - inv_density * d_radial[4] + viscous[2], -convect[3] - current[2] * (radial_grad[3] + swirl_vel * inverse_r) - inv_density * azimuth * turned[4] + viscous[3], -convect[4] - heat_ratio * pressure * divergence - current[1] * axial_grad[4] - current[2] * radial_grad[4]]
        new_parts = [current[comp_idx] + pseudo_step * (tendency[comp_idx] + frequency * turned[comp_idx] - damping * current[comp_idx] + drive[part_idx, comp_idx]) for comp_idx in range(5)]
        outputs.append(jnp.stack(new_parts, axis=-3))
    return jnp.stack(outputs, axis=-4)

def stress_terms(state_now):
    axial_re, axial_im = (state_now[..., 0, 1, :, :], state_now[..., 1, 1, :, :])
    radial_re, radial_im = (state_now[..., 0, 2, :, :], state_now[..., 1, 2, :, :])
    swirl_re, swirl_im = (state_now[..., 0, 3, :, :], state_now[..., 1, 3, :, :])
    return jnp.stack([axial_re * axial_re + axial_im * axial_im, axial_re * radial_re + axial_im * radial_im, radial_re * radial_re + radial_im * radial_im, swirl_re * swirl_re + swirl_im * swirl_im], axis=-3)

def correction_terms(stress_ext, mean_ext, viscosity, inverse_r):
    center = stress_ext[:, 2:-2, :]
    stress_ax = axial_diff(stress_ext)
    stress_rad = radial_diff(center)
    force_axial = -(stress_ax[0] + stress_rad[1] + center[1] * inverse_r)
    force_radial = -(stress_ax[1] + stress_rad[2] + (center[2] - center[3]) * inverse_r)
    mean_center = mean_ext[:, 2:-2, :]
    lap_axial = axial_second(mean_ext[1]) + radial_second(mean_center[1])
    lap_radial = axial_second(mean_ext[2]) + radial_second(mean_center[2])
    return jnp.stack([force_axial + viscosity * lap_axial, force_radial + viscosity * lap_radial])

def reference(forced_pairs, cell_type, mean_density, mean_velocity, mean_pressure, eddy_visc, forcing):
    inverse_r = 1.0 / (jnp.arange(NR, dtype=jnp.float32) + 0.5)
    envelope = 0.5 + (jnp.arange(NXT, dtype=jnp.float32) + 0.5) / NXT
    drive = forcing * envelope[:, None]
    damping = 2.0 * (cell_type == 1).astype(jnp.float32) + 10.0 * (cell_type == 2).astype(jnp.float32)
    mean_field = jnp.stack([mean_density, mean_velocity[0], mean_velocity[1], mean_velocity[2], mean_pressure])
    mean_ext = jnp.pad(mean_field, ((0, 0), (2, 2), (0, 0)))
    coeffs = coefficients(mean_ext, eddy_visc, damping, inverse_r)

    def one_pair(stress_sum, pair_row):
        frequency = 0.05 * pair_row[0].astype(jnp.float32)
        wavenumber = pair_row[1].astype(jnp.float32)
        state_now = drive
        for sweep_idx in range(SWEEPS):
            padded = jnp.pad(state_now, ((0, 0), (0, 0), (2, 2), (0, 0)))
            state_now = sweep(padded, coeffs, wavenumber, frequency, drive)
        return (stress_sum + stress_terms(state_now), state_now)
    stress_sum, responses = lax.scan(one_pair, jnp.zeros((4, NXT, NR), jnp.float32), forced_pairs)
    stress_ext = jnp.pad(stress_sum / PAIRS, ((0, 0), (2, 2), (0, 0)))
    increment = correction_terms(stress_ext, mean_ext, eddy_visc, inverse_r)
    spread = jnp.sqrt(jnp.mean(increment * increment) + 1e-06)
    return (responses, increment / spread)
```

```python
import functools

import jax
import jax.numpy as jnp
from jax import lax
from jax.experimental import pallas as pl
from jax.experimental.pallas import tpu as pltpu
from jax.sharding import PartitionSpec as P

HEAT_RATIO = 1.4
STEP = 0.1
WAVES = 5
HALO = 8
LANES = 128
F32 = jnp.float32


def exchange_kernel(count, rows, forcing, density, velocity, pressure, visc, cells, halo, halo_cells, send, recv):
    me = lax.axis_index("axial")
    has_low, has_high = me > 0, me < count - 1
    barrier = pltpu.get_barrier_semaphore()

    @pl.when(has_low)
    def _():
        pl.semaphore_signal(barrier, inc=1, device_id={"axial": me - 1}, device_id_type=pl.DeviceIdType.MESH)

    @pl.when(has_high)
    def _():
        pl.semaphore_signal(barrier, inc=1, device_id={"axial": me + 1}, device_id_type=pl.DeviceIdType.MESH)

    @pl.when(has_low & has_high)
    def _():
        pl.semaphore_wait(barrier, 2)

    @pl.when((me == 0) | (me == count - 1))
    def _():
        pl.semaphore_wait(barrier, 1)

    def copies(side):
        start = rows - HALO if side == 0 else 0
        target = me + 1 if side == 0 else me - 1
        cut = pl.ds(start, HALO)
        moves = [
            (forcing.at[:, cut, :], halo.at[side, pl.ds(0, 10)]),
            (velocity.at[:, cut, :], halo.at[side, pl.ds(11, 3)]),
            (density.at[cut, :], halo.at[side, 10]),
            (pressure.at[cut, :], halo.at[side, 14]),
            (visc.at[cut, :], halo.at[side, 15]),
            (cells.at[cut, :], halo_cells.at[side]),
        ]
        return [
            pltpu.make_async_remote_copy(
                src_ref=src,
                dst_ref=dst,
                send_sem=send.at[side, index],
                recv_sem=recv.at[side, index],
                device_id={"axial": target},
                device_id_type=pl.DeviceIdType.MESH,
            )
            for index, (src, dst) in enumerate(moves)
        ]

    up, down = copies(0), copies(1)

    @pl.when(has_high)
    def _():
        for copy in up:
            copy.start()

    @pl.when(has_low)
    def _():
        for copy in down:
            copy.start()

    @pl.when(has_high)
    def _():
        for copy in up:
            copy.wait_send()
        for copy in down:
            copy.wait_recv()

    @pl.when(has_low)
    def _():
        for copy in down:
            copy.wait_send()
        for copy in up:
            copy.wait_recv()


def exchange(count, forcing, density, velocity, pressure, visc, cells):
    rows, radial = density.shape
    return pl.pallas_call(
        functools.partial(exchange_kernel, count, rows),
        out_shape=(
            jax.ShapeDtypeStruct((2, 16, HALO, radial), F32),
            jax.ShapeDtypeStruct((2, HALO, radial), jnp.int32),
        ),
        in_specs=[pl.BlockSpec(memory_space=pl.ANY)] * 6,
        out_specs=(pl.BlockSpec(memory_space=pl.ANY), pl.BlockSpec(memory_space=pl.ANY)),
        scratch_shapes=[pltpu.SemaphoreType.DMA((2, 6)), pltpu.SemaphoreType.DMA((2, 6))],
        compiler_params=pltpu.CompilerParams(collective_id=0, has_side_effects=True),
    )(forcing, density, velocity, pressure, visc, cells)


def response_kernel(
    count, rows, blocks, pairs, forced, forcing, density, velocity, pressure, visc, cells, halo, halo_cells,
    responses, increment, squares,
    field, kind, first, stress, table_p, table_r, result, in_sem, out_sem,
):
    me = lax.axis_index("axial")
    all_rows = rows * count
    ext = rows + 2 * HALO
    own = pl.ds(HALO, rows)

    moves = []
    for block in range(blocks):
        lanes = pl.ds(block * LANES, LANES)
        moves += [
            (forcing.at[:, :, lanes], field.at[pl.ds(0, 10), block + 1, own]),
            (velocity.at[:, :, lanes], field.at[pl.ds(11, 3), block + 1, own]),
            (density.at[:, lanes], field.at[10, block + 1, own]),
            (pressure.at[:, lanes], field.at[14, block + 1, own]),
            (visc.at[:, lanes], field.at[15, block + 1, own]),
            (cells.at[:, lanes], kind.at[block + 1, own]),
        ]
        for side, start in ((0, 0), (1, HALO + rows)):
            edge = pl.ds(start, HALO)
            moves += [
                (halo.at[side, :, :, lanes], field.at[:, block + 1, edge]),
                (halo_cells.at[side, :, lanes], kind.at[block + 1, edge]),
            ]
    copies = [pltpu.make_async_copy(src, dst, in_sem.at[i]) for i, (src, dst) in enumerate(moves)]
    for copy in copies:
        copy.start()
    for side in (0, blocks + 1):
        field[:, side] = jnp.zeros((16, ext, LANES), F32)
        first[:, side] = jnp.zeros((26, ext, LANES), F32)
        stress[:, side] = jnp.zeros((4, ext, LANES), F32)
    for copy in copies:
        copy.wait()

    @pl.when(me == 0)
    def _():
        field[:, :, pl.ds(0, HALO)] = jnp.zeros((16, blocks + 2, HALO, LANES), F32)
        kind[:, pl.ds(0, HALO)] = jnp.zeros((blocks + 2, HALO, LANES), jnp.int32)

    @pl.when(me == count - 1)
    def _():
        field[:, :, pl.ds(HALO + rows, HALO)] = jnp.zeros((16, blocks + 2, HALO, LANES), F32)
        kind[:, pl.ds(HALO + rows, HALO)] = jnp.zeros((blocks + 2, HALO, LANES), jnp.int32)

    lane = lax.broadcasted_iota(jnp.int32, (8, LANES), 1)
    sub = lax.broadcasted_iota(jnp.int32, (8, LANES), 0)
    is_first, is_last = lane == 0, lane == LANES - 1

    def global_row(start):
        return sub + (me * rows + (start - HALO))

    def inside(start):
        row = global_row(start)
        return jnp.where((row >= 0) & (row < all_rows), 1.0, 0.0).astype(F32)

    def inverse_r(c):
        return 1.0 / (((c - 1) * LANES + lane).astype(F32) + 0.5)

    def scale_drive(c, carry):
        for start in range(0, ext, 8):
            envelope = 0.5 + (global_row(start).astype(F32) + 0.5) / all_rows
            for index in range(10):
                field[index, c, pl.ds(start, 8)] = field[index, c, pl.ds(start, 8)] * envelope
        return carry

    lax.fori_loop(1, blocks + 1, scale_drive, 0)

    def at(ref, index, c, start):
        return ref[index, c, pl.ds(start, 8)]

    def axial(ref, index, c, start):
        return [at(ref, index, c, start + offset) for offset in (-2, -1, 1, 2)]

    def radial(ref, index, c, start):
        here = at(ref, index, c, start)
        left = pltpu.roll(jnp.where(is_last, at(ref, index, c - 1, start), here), 1, 1)
        right = pltpu.roll(jnp.where(is_first, at(ref, index, c + 1, start), here), LANES - 1, 1)
        return left, right

    def twelve(near):
        return (near[0] - near[3]) + 8.0 * (near[2] - near[1])

    def coefficients(c, start):
        k = {}
        rho, u, v, w, p = [at(field, 10 + i, c, start) for i in range(5)]
        ir = inverse_r(c)
        nu = STEP * at(field, 15, c, start)
        cell = kind[c, pl.ds(start, 8)]
        damp = jnp.where(cell == 1, 2.0, jnp.where(cell == 2, 10.0, 0.0)).astype(F32)
        inv_rho = STEP / jnp.where(rho > 0.0, rho, 1.0)
        for i in range(5):
            left, right = radial(field, 10 + i, c, start)
            k["x", i] = (-STEP / 12.0) * twelve(axial(field, 10 + i, c, start))
            k["r", i] = (-STEP / 2.0) * (right - left)
        swirl = w * ir
        k["r", 3] = k["r", 3] - STEP * swirl
        k["swirl2"] = (2.0 * STEP) * swirl
        k["u12"] = (-STEP / 12.0) * u
        k["v2"] = (-STEP / 2.0) * v
        k["inviscid"] = 1.0 - STEP * damp
        nu12 = nu * (1.0 / 12.0)
        k["viscous"] = k["inviscid"] - nu * 4.5
        k["m2"] = k["u12"] - nu12
        k["m1"] = 16.0 * nu12 - 8.0 * k["u12"]
        k["p1"] = 16.0 * nu12 + 8.0 * k["u12"]
        k["p2"] = -nu12 - k["u12"]
        slope = 0.5 * nu * ir + k["v2"]
        k["left"] = nu - slope
        k["right"] = nu + slope
        k["rho_div"] = -STEP * rho
        k["p_div"] = (-STEP * HEAT_RATIO) * p
        k["px"] = inv_rho * (-1.0 / 12.0)
        k["pr"] = inv_rho * -0.5
        k["ir"] = ir
        k["turn"] = -STEP * swirl
        k["turn_rho"] = -STEP * rho * ir
        k["turn_w"] = -inv_rho * ir
        k["turn_p"] = k["p_div"] * ir
        k["square"] = -nu * ir * ir
        return k

    def base_operator(k, ref, ids, c, start):
        value, ax, rad = {}, {}, {}
        for i in range(5):
            if ids[i] is not None:
                value[i] = at(ref, ids[i], c, start)
                ax[i] = axial(ref, ids[i], c, start)
                rad[i] = radial(ref, ids[i], c, start)
        div = (1.0 / 12.0) * twelve(ax[1]) + 0.5 * (rad[2][1] - rad[2][0]) + value[2] * k["ir"]
        out = []
        for i in range(5):
            if i in (0, 4):
                term = k["rho_div" if i == 0 else "p_div"] * div
                if i in value:
                    term = term + k["inviscid"] * value[i] + k["u12"] * twelve(ax[i]) + k["v2"] * (rad[i][1] - rad[i][0])
            else:
                term = (
                    k["viscous"] * value[i]
                    + (k["m2"] * ax[i][0] + k["m1"] * ax[i][1])
                    + (k["p1"] * ax[i][2] + k["p2"] * ax[i][3])
                    + (k["left"] * rad[i][0] + k["right"] * rad[i][1])
                )
            if i != 3:
                term = term + k["x", i] * value[1]
            term = term + k["r", i] * value[2]
            if i == 1 and 4 in value:
                term = term + k["px"] * twelve(ax[4])
            if i == 2:
                term = term + k["swirl2"] * value[3]
                if 4 in value:
                    term = term + k["pr"] * (rad[4][1] - rad[4][0])
            out.append(term)
        return out

    def turn_operator(k, q):
        out = [None] * 5
        for i in range(5):
            if q[i] is not None:
                out[i] = k["turn"] * q[i]
        for i, source, name in ((0, 3, "turn_rho"), (3, 4, "turn_w"), (4, 3, "turn_p")):
            if q[source] is not None:
                extra = k[name] * q[source]
                out[i] = extra if out[i] is None else out[i] + extra
        return out

    def base(k, ref, ids, c, start):
        out = base_operator(k, ref, ids, c, start)
        return out

    def first_stage(c, carry):
        for start in range(4, rows + 2 * HALO - 4, 8):
            k = coefficients(c, start)
            keep = inside(start)
            for part in range(2):
                d = [at(field, part * 5 + i, c, start) for i in range(5)]
                moved = base(k, field, [part * 5 + i for i in range(5)], c, start)
                turned = turn_operator(k, d)
                for i in range(5):
                    first[part * 5 + i, c, pl.ds(start, 8)] = keep * (moved[i] + STEP * d[i])
                    first[10 + part * 5 + i, c, pl.ds(start, 8)] = keep * turned[i]
                for i in range(1, 4):
                    first[20 + part * 3 + i - 1, c, pl.ds(start, 8)] = keep * (k["square"] * d[i])
        return carry

    lax.fori_loop(1, blocks + 1, first_stage, 0)

    def tables(c, start):
        k = coefficients(c, start)
        window = pl.ds(start, 8)
        for part in range(2):
            other = 1 - part
            sign = -1.0 if part == 0 else 1.0
            h0 = [part * 5 + i for i in range(5)]
            h0_o = [other * 5 + i for i in range(5)]
            h1 = [10 + part * 5 + i for i in range(5)]
            h1_o = [10 + other * 5 + i for i in range(5)]
            h2 = [None] + [20 + part * 3 + i for i in range(3)] + [None]
            h2_o = [None] + [20 + other * 3 + i for i in range(3)] + [None]

            def values(ids):
                return [None if i is None else at(first, i, c, start) for i in ids]

            d = [at(field, part * 5 + i, c, start) for i in range(5)]
            v0, v0_o, v1, v1_o, v2, v2_o = [values(ids) for ids in (h0, h0_o, h1, h1_o, h2, h2_o)]
            e0 = base(k, first, h0, c, start)
            e1 = base(k, first, h1_o, c, start)
            e2 = base(k, first, h2, c, start)
            t0 = turn_operator(k, v0_o)
            t1 = turn_operator(k, v1)
            t2 = turn_operator(k, v2_o)
            for i in range(5):
                a0 = e0[i] + STEP * d[i]
                a1 = e1[i] + t0[i]
                a2 = e2[i] - t1[i]
                a3 = t2[i]
                a4 = None
                if v2[i] is not None:
                    a2 = a2 + k["square"] * v0[i]
                    a3 = a3 + k["square"] * v1_o[i]
                    a4 = k["square"] * v2[i]
                r0 = 2.0 * v0[i] - STEP * d[i]
                for m in range(WAVES):
                    if m == 0:
                        p_m, r_m = a0, r0
                    else:
                        even = a2 if a4 is None else a2 + float(m * m) * a4
                        odd = a1 + float(m * m) * a3
                        p_m = a0 + float(m * m) * even + (sign * m) * odd
                        r_m = r0 + (sign * 2.0 * m) * v1_o[i]
                        if v2[i] is not None:
                            r_m = r_m + float(2 * m * m) * v2[i]
                    table_p[m, part * 5 + i, window] = p_m
                    table_r[m, part * 5 + i, window] = r_m

    def expand(c, start):
        window = pl.ds(start, 8)
        d = [field[i, c, window] for i in range(10)]

        def one(pair, sums):
            alpha = (STEP * 0.05) * forced[pair, 0].astype(F32)
            m = forced[pair, 1]
            square = alpha * alpha
            q = []
            for i in range(10):
                other = (i + 5) % 10
                turned = alpha * table_r[m, other, window]
                even = table_p[m, i, window] - square * d[i]
                q.append(even - turned if i < 5 else even + turned)
            for i in range(10):
                result[c - 1, pair, i, window] = q[i]
            return (
                sums[0] + (q[1] * q[1] + q[6] * q[6]),
                sums[1] + (q[1] * q[2] + q[6] * q[7]),
                sums[2] + (q[2] * q[2] + q[7] * q[7]),
                sums[3] + (q[3] * q[3] + q[8] * q[8]),
            )

        zero = jnp.zeros((8, LANES), F32)
        sums = lax.fori_loop(0, pairs, one, (zero,) * 4, unroll=2)
        keep = inside(start) * (1.0 / pairs)
        for i in range(4):
            stress[i, c, window] = jnp.where(keep > 0.0, sums[i] * keep, 0.0)

    def out_copy(c):
        lanes = pl.ds(pl.multiple_of((c - 1) * LANES, LANES), LANES)
        return pltpu.make_async_copy(result.at[c - 1, :, :, own], responses.at[:, :, :, lanes], out_sem.at[c - 1])

    def second_stage(c, carry):
        for start in range(6, rows + HALO + 2, 8):
            tables(c, start)
        for start in range(6, rows + HALO + 2, 8):
            expand(c, start)
        out_copy(c).start()
        return carry

    lax.fori_loop(1, blocks + 1, second_stage, 0)

    total = jnp.zeros((8, LANES), F32)
    for c in range(1, blocks + 1):
        ir = inverse_r(c)
        for start in range(HALO, HALO + rows, 8):
            nu = at(field, 15, c, start)

            def laplace(index):
                near = axial(field, index, c, start)
                left, right = radial(field, index, c, start)
                here = at(field, index, c, start)
                second = (16.0 * (near[1] + near[2]) - (near[0] + near[3]) - 30.0 * here) * (1.0 / 12.0)
                return second + (right - 2.0 * here + left)

            def along(index):
                return (1.0 / 12.0) * twelve(axial(stress, index, c, start))

            def across(index):
                left, right = radial(stress, index, c, start)
                return 0.5 * (right - left)

            s1, s2, s3 = [at(stress, i, c, start) for i in (1, 2, 3)]
            first_part = nu * laplace(11) - (along(0) + across(1) + s1 * ir)
            second_part = nu * laplace(12) - (along(1) + across(2) + (s2 - s3) * ir)
            place = (pl.ds(start - HALO, 8), pl.ds((c - 1) * LANES, LANES))
            increment[(0,) + place] = first_part
            increment[(1,) + place] = second_part
            total = total + (first_part * first_part + second_part * second_part)
    squares[...] = total
    for c in range(1, blocks + 1):
        out_copy(c).wait()


def respond(count, forced, forcing, density, velocity, pressure, visc, cells, halo, halo_cells):
    rows, radial = density.shape
    pairs = forced.shape[0]
    blocks = radial // LANES
    ext = rows + 2 * HALO
    anywhere = pl.BlockSpec(memory_space=pl.ANY)
    vmem = pl.BlockSpec(memory_space=pltpu.VMEM)
    return pl.pallas_call(
        functools.partial(response_kernel, count, rows, blocks, pairs),
        out_shape=(
            jax.ShapeDtypeStruct((pairs, 10, rows, radial), F32),
            jax.ShapeDtypeStruct((2, rows, radial), F32),
            jax.ShapeDtypeStruct((8, LANES), F32),
        ),
        in_specs=[pl.BlockSpec(memory_space=pltpu.SMEM)] + [anywhere] * 8,
        out_specs=(anywhere, vmem, vmem),
        scratch_shapes=[
            pltpu.VMEM((16, blocks + 2, ext, LANES), F32),
            pltpu.VMEM((blocks + 2, ext, LANES), jnp.int32),
            pltpu.VMEM((26, blocks + 2, ext, LANES), F32),
            pltpu.VMEM((4, blocks + 2, ext, LANES), F32),
            pltpu.VMEM((WAVES, 10, ext, LANES), F32),
            pltpu.VMEM((WAVES, 10, ext, LANES), F32),
            pltpu.VMEM((blocks, pairs, 10, ext, LANES), F32),
            pltpu.SemaphoreType.DMA((blocks * 10,)),
            pltpu.SemaphoreType.DMA((blocks,)),
        ],
        compiler_params=pltpu.CompilerParams(vmem_limit_bytes=50 * 1024 * 1024),
    )(forced, forcing, density, velocity, pressure, visc, cells, halo, halo_cells)


def total_kernel(count, cells, squares, spread, parts, send, recv):
    me = lax.axis_index("axial")
    barrier = pltpu.get_barrier_semaphore()
    others = [lax.rem(me + hop, count) for hop in range(1, count)]
    for other in others:
        pl.semaphore_signal(barrier, inc=1, device_id={"axial": other}, device_id_type=pl.DeviceIdType.MESH)
    pl.semaphore_wait(barrier, count - 1)
    copies = [
        pltpu.make_async_remote_copy(
            src_ref=squares,
            dst_ref=parts.at[hop],
            send_sem=send.at[hop],
            recv_sem=recv.at[hop],
            device_id={"axial": other},
            device_id_type=pl.DeviceIdType.MESH,
        )
        for hop, other in enumerate(others)
    ]
    for copy in copies:
        copy.start()
    for copy in copies:
        copy.wait()
    total = squares[...]
    for hop in range(count - 1):
        total = total + parts[hop]
    total = jnp.sum(jnp.sum(total, axis=1, keepdims=True), axis=0, keepdims=True)
    spread[...] = jnp.broadcast_to(jnp.sqrt(total / cells + 1e-06), (8, LANES))


def spread_of(count, cells, squares):
    vmem = pl.BlockSpec(memory_space=pltpu.VMEM)
    return pl.pallas_call(
        functools.partial(total_kernel, count, cells),
        out_shape=jax.ShapeDtypeStruct((8, LANES), F32),
        in_specs=[vmem],
        out_specs=vmem,
        scratch_shapes=[
            pltpu.VMEM((count - 1, 8, LANES), F32),
            pltpu.SemaphoreType.DMA((count - 1,)),
            pltpu.SemaphoreType.DMA((count - 1,)),
        ],
        compiler_params=pltpu.CompilerParams(collective_id=1, has_side_effects=True),
    )(squares)


def shards(count, forced, cells, density, velocity, pressure, visc, forcing):
    rows, radial = density.shape
    pairs = forced.shape[0]
    drive = forcing.reshape(10, rows, radial)
    halo, halo_cells = exchange(count, drive, density, velocity, pressure, visc, cells)
    responses, increment, squares = respond(
        count, forced, drive, density, velocity, pressure, visc, cells, halo, halo_cells
    )
    spread = spread_of(count, 2 * rows * count * radial, squares)
    return (responses.reshape(pairs, 2, 5, rows, radial), increment / spread[0, 0])


def solution(mesh):
    placed = (
        P("case", None),
        P(("case", "axial"), None),
        P(("case", "axial"), None),
        P("case", "axial", None),
        P(("case", "axial"), None),
        P(("case", "axial"), None),
        P("case", None, "axial", None),
    )
    return jax.shard_map(
        functools.partial(shards, mesh.shape["axial"]),
        mesh=mesh,
        in_specs=placed,
        out_specs=(P("case", None, None, "axial", None), P("case", "axial", None)),
        check_vma=False,
    )
```

```python
import functools

import jax
import jax.numpy as jnp
from jax import lax
from jax.experimental import pallas as pl
from jax.experimental.pallas import tpu as pltpu
from jax.sharding import PartitionSpec as P

HEAT_RATIO = 1.4
STEP = 0.1
WAVES = 5
HALO = 8
WIDE = 6
NARROW = 4
LANES = 128
F32 = jnp.float32


def exchange_kernel(count, rows, forcing, density, velocity, pressure, visc, cells, halo, halo_cells, send, recv):
    me = lax.axis_index("axial")
    has_low, has_high = me > 0, me < count - 1
    barrier = pltpu.get_barrier_semaphore()

    @pl.when(has_low)
    def _():
        pl.semaphore_signal(barrier, inc=1, device_id={"axial": me - 1}, device_id_type=pl.DeviceIdType.MESH)

    @pl.when(has_high)
    def _():
        pl.semaphore_signal(barrier, inc=1, device_id={"axial": me + 1}, device_id_type=pl.DeviceIdType.MESH)

    @pl.when(has_low & has_high)
    def _():
        pl.semaphore_wait(barrier, 2)

    @pl.when((me == 0) | (me == count - 1))
    def _():
        pl.semaphore_wait(barrier, 1)

    def copies(side):
        target = me + 1 if side == 0 else me - 1

        def cut(reach):
            return pl.ds(rows - reach if side == 0 else 0, reach)

        def to(reach):
            return pl.ds(HALO - reach if side == 0 else 0, reach)

        moves = [
            (forcing.at[:, cut(WIDE), :], halo.at[side, pl.ds(0, 10), to(WIDE)]),
            (velocity.at[:, cut(WIDE), :], halo.at[side, pl.ds(11, 3), to(WIDE)]),
            (density.at[cut(WIDE), :], halo.at[side, 10, to(WIDE)]),
            (pressure.at[cut(WIDE), :], halo.at[side, 14, to(WIDE)]),
            (visc.at[cut(NARROW), :], halo.at[side, 15, to(NARROW)]),
            (cells.at[cut(NARROW), :], halo_cells.at[side, to(NARROW)]),
        ]
        return [
            pltpu.make_async_remote_copy(
                src_ref=src,
                dst_ref=dst,
                send_sem=send.at[side, index],
                recv_sem=recv.at[side, index],
                device_id={"axial": target},
                device_id_type=pl.DeviceIdType.MESH,
            )
            for index, (src, dst) in enumerate(moves)
        ]

    up, down = copies(0), copies(1)

    @pl.when(has_high)
    def _():
        for copy in up:
            copy.start()

    @pl.when(has_low)
    def _():
        for copy in down:
            copy.start()

    @pl.when(has_high)
    def _():
        for copy in up:
            copy.wait_send()
        for copy in down:
            copy.wait_recv()

    @pl.when(has_low)
    def _():
        for copy in down:
            copy.wait_send()
        for copy in up:
            copy.wait_recv()


def exchange(count, forcing, density, velocity, pressure, visc, cells):
    rows, radial = density.shape
    return pl.pallas_call(
        functools.partial(exchange_kernel, count, rows),
        out_shape=(
            jax.ShapeDtypeStruct((2, 16, HALO, radial), F32),
            jax.ShapeDtypeStruct((2, HALO, radial), jnp.int32),
        ),
        in_specs=[pl.BlockSpec(memory_space=pl.ANY)] * 6,
        out_specs=(pl.BlockSpec(memory_space=pl.ANY), pl.BlockSpec(memory_space=pl.ANY)),
        scratch_shapes=[pltpu.SemaphoreType.DMA((2, 6)), pltpu.SemaphoreType.DMA((2, 6))],
        compiler_params=pltpu.CompilerParams(collective_id=0, has_side_effects=True),
    )(forcing, density, velocity, pressure, visc, cells)


def response_kernel(
    count, rows, blocks, pairs, forced, forcing, density, velocity, pressure, visc, cells, halo, halo_cells,
    responses, increment_out, squares_out,
    increment, squares, field, kind, first, stress, table_p, table_r, result, in_sem, out_sem, end_sem,
):
    me = lax.axis_index("axial")
    all_rows = rows * count
    ext = rows + 2 * HALO
    own = pl.ds(HALO, rows)

    moves = []
    for block in range(blocks):
        lanes = pl.ds(block * LANES, LANES)
        moves += [
            (forcing.at[:, :, lanes], field.at[pl.ds(0, 10), block + 1, own]),
            (velocity.at[:, :, lanes], field.at[pl.ds(11, 3), block + 1, own]),
            (density.at[:, lanes], field.at[10, block + 1, own]),
            (pressure.at[:, lanes], field.at[14, block + 1, own]),
            (visc.at[:, lanes], field.at[15, block + 1, own]),
            (cells.at[:, lanes], kind.at[block + 1, own]),
        ]
        for side, start in ((0, 0), (1, HALO + rows)):
            edge = pl.ds(start, HALO)
            moves += [
                (halo.at[side, :, :, lanes], field.at[:, block + 1, edge]),
                (halo_cells.at[side, :, lanes], kind.at[block + 1, edge]),
            ]
    copies = [pltpu.make_async_copy(src, dst, in_sem.at[i]) for i, (src, dst) in enumerate(moves)]
    for copy in copies:
        copy.start()
    for side in (0, blocks + 1):
        field[:, side] = jnp.zeros((16, ext, LANES), F32)
        first[:, side] = jnp.zeros((26, ext, LANES), F32)
        stress[:, side] = jnp.zeros((4, ext, LANES), F32)
    for copy in copies:
        copy.wait()

    @pl.when(me == 0)
    def _():
        field[:, :, pl.ds(0, HALO)] = jnp.zeros((16, blocks + 2, HALO, LANES), F32)
        kind[:, pl.ds(0, HALO)] = jnp.zeros((blocks + 2, HALO, LANES), jnp.int32)

    @pl.when(me == count - 1)
    def _():
        field[:, :, pl.ds(HALO + rows, HALO)] = jnp.zeros((16, blocks + 2, HALO, LANES), F32)
        kind[:, pl.ds(HALO + rows, HALO)] = jnp.zeros((blocks + 2, HALO, LANES), jnp.int32)

    lane = lax.broadcasted_iota(jnp.int32, (8, LANES), 1)
    sub = lax.broadcasted_iota(jnp.int32, (8, LANES), 0)
    is_first, is_last = lane == 0, lane == LANES - 1

    def global_row(start):
        return sub + (me * rows + (start - HALO))

    def inside(start):
        row = global_row(start)
        return jnp.where((row >= 0) & (row < all_rows), 1.0, 0.0).astype(F32)

    def inverse_r(c):
        return 1.0 / (((c - 1) * LANES + lane).astype(F32) + 0.5)

    def scale_drive(c, carry):
        for start in range(0, ext, 8):
            envelope = 0.5 + (global_row(start).astype(F32) + 0.5) / all_rows
            for index in range(10):
                field[index, c, pl.ds(start, 8)] = field[index, c, pl.ds(start, 8)] * envelope
        return carry

    lax.fori_loop(1, blocks + 1, scale_drive, 0)

    def at(ref, index, c, start):
        return ref[index, c, pl.ds(start, 8)]

    def axial(ref, index, c, start):
        return [at(ref, index, c, start + offset) for offset in (-2, -1, 1, 2)]

    def radial(ref, index, c, start):
        here = at(ref, index, c, start)
        left = pltpu.roll(jnp.where(is_last, at(ref, index, c - 1, start), here), 1, 1)
        right = pltpu.roll(jnp.where(is_first, at(ref, index, c + 1, start), here), LANES - 1, 1)
        return left, right

    def twelve(near):
        return (near[0] - near[3]) + 8.0 * (near[2] - near[1])

    def coefficients(c, start):
        k = {}
        rho, u, v, w, p = [at(field, 10 + i, c, start) for i in range(5)]
        ir = inverse_r(c)
        nu = STEP * at(field, 15, c, start)
        cell = kind[c, pl.ds(start, 8)]
        damp = jnp.where(cell == 1, 2.0, jnp.where(cell == 2, 10.0, 0.0)).astype(F32)
        inv_rho = STEP / jnp.where(rho > 0.0, rho, 1.0)
        for i in range(5):
            left, right = radial(field, 10 + i, c, start)
            k["x", i] = (-STEP / 12.0) * twelve(axial(field, 10 + i, c, start))
            k["r", i] = (-STEP / 2.0) * (right - left)
        swirl = w * ir
        k["r", 3] = k["r", 3] - STEP * swirl
        k["swirl2"] = (2.0 * STEP) * swirl
        k["u12"] = (-STEP / 12.0) * u
        k["v2"] = (-STEP / 2.0) * v
        k["inviscid"] = 1.0 - STEP * damp
        nu12 = nu * (1.0 / 12.0)
        k["viscous"] = k["inviscid"] - nu * 4.5
        k["m2"] = k["u12"] - nu12
        k["m1"] = 16.0 * nu12 - 8.0 * k["u12"]
        k["p1"] = 16.0 * nu12 + 8.0 * k["u12"]
        k["p2"] = -nu12 - k["u12"]
        slope = 0.5 * nu * ir + k["v2"]
        k["left"] = nu - slope
        k["right"] = nu + slope
        k["rho_div"] = -STEP * rho
        k["p_div"] = (-STEP * HEAT_RATIO) * p
        k["px"] = inv_rho * (-1.0 / 12.0)
        k["pr"] = inv_rho * -0.5
        k["ir"] = ir
        k["turn"] = -STEP * swirl
        k["turn_rho"] = -STEP * rho * ir
        k["turn_w"] = -inv_rho * ir
        k["turn_p"] = k["p_div"] * ir
        k["square"] = -nu * ir * ir
        return k

    def base_operator(k, ref, ids, c, start):
        value, ax, rad = {}, {}, {}
        for i in range(5):
            if ids[i] is not None:
                value[i] = at(ref, ids[i], c, start)
                ax[i] = axial(ref, ids[i], c, start)
                rad[i] = radial(ref, ids[i], c, start)
        div = (1.0 / 12.0) * twelve(ax[1]) + 0.5 * (rad[2][1] - rad[2][0]) + value[2] * k["ir"]
        out = []
        for i in range(5):
            if i in (0, 4):
                term = k["rho_div" if i == 0 else "p_div"] * div
                if i in value:
                    term = term + k["inviscid"] * value[i] + k["u12"] * twelve(ax[i]) + k["v2"] * (rad[i][1] - rad[i][0])
            else:
                term = (
                    k["viscous"] * value[i]
                    + (k["m2"] * ax[i][0] + k["m1"] * ax[i][1])
                    + (k["p1"] * ax[i][2] + k["p2"] * ax[i][3])
                    + (k["left"] * rad[i][0] + k["right"] * rad[i][1])
                )
            if i != 3:
                term = term + k["x", i] * value[1]
            term = term + k["r", i] * value[2]
            if i == 1 and 4 in value:
                term = term + k["px"] * twelve(ax[4])
            if i == 2:
                term = term + k["swirl2"] * value[3]
                if 4 in value:
                    term = term + k["pr"] * (rad[4][1] - rad[4][0])
            out.append(term)
        return out

    def turn_operator(k, q):
        out = [None] * 5
        for i in range(5):
            if q[i] is not None:
                out[i] = k["turn"] * q[i]
        for i, source, name in ((0, 3, "turn_rho"), (3, 4, "turn_w"), (4, 3, "turn_p")):
            if q[source] is not None:
                extra = k[name] * q[source]
                out[i] = extra if out[i] is None else out[i] + extra
        return out

    def base(k, ref, ids, c, start):
        out = base_operator(k, ref, ids, c, start)
        return out

    def first_stage(c, carry):
        for start in range(4, rows + 2 * HALO - 4, 8):
            k = coefficients(c, start)
            keep = inside(start)
            for part in range(2):
                d = [at(field, part * 5 + i, c, start) for i in range(5)]
                moved = base(k, field, [part * 5 + i for i in range(5)], c, start)
                turned = turn_operator(k, d)
                for i in range(5):
                    first[part * 5 + i, c, pl.ds(start, 8)] = keep * (moved[i] + STEP * d[i])
                    first[10 + part * 5 + i, c, pl.ds(start, 8)] = keep * turned[i]
                for i in range(1, 4):
                    first[20 + part * 3 + i - 1, c, pl.ds(start, 8)] = keep * (k["square"] * d[i])
        return carry

    lax.fori_loop(1, blocks + 1, first_stage, 0)

    def tables(c, start):
        k = coefficients(c, start)
        window = pl.ds(start, 8)
        for part in range(2):
            other = 1 - part
            sign = -1.0 if part == 0 else 1.0
            h0 = [part * 5 + i for i in range(5)]
            h0_o = [other * 5 + i for i in range(5)]
            h1 = [10 + part * 5 + i for i in range(5)]
            h1_o = [10 + other * 5 + i for i in range(5)]
            h2 = [None] + [20 + part * 3 + i for i in range(3)] + [None]
            h2_o = [None] + [20 + other * 3 + i for i in range(3)] + [None]

            def values(ids):
                return [None if i is None else at(first, i, c, start) for i in ids]

            d = [at(field, part * 5 + i, c, start) for i in range(5)]
            v0, v0_o, v1, v1_o, v2, v2_o = [values(ids) for ids in (h0, h0_o, h1, h1_o, h2, h2_o)]
            e0 = base(k, first, h0, c, start)
            e1 = base(k, first, h1_o, c, start)
            e2 = base(k, first, h2, c, start)
            t0 = turn_operator(k, v0_o)
            t1 = turn_operator(k, v1)
            t2 = turn_operator(k, v2_o)
            for i in range(5):
                a0 = e0[i] + STEP * d[i]
                a1 = e1[i] + t0[i]
                a2 = e2[i] - t1[i]
                a3 = t2[i]
                a4 = None
                if v2[i] is not None:
                    a2 = a2 + k["square"] * v0[i]
                    a3 = a3 + k["square"] * v1_o[i]
                    a4 = k["square"] * v2[i]
                r0 = 2.0 * v0[i] - STEP * d[i]
                for m in range(WAVES):
                    if m == 0:
                        p_m, r_m = a0, r0
                    else:
                        even = a2 if a4 is None else a2 + float(m * m) * a4
                        odd = a1 + float(m * m) * a3
                        p_m = a0 + float(m * m) * even + (sign * m) * odd
                        r_m = r0 + (sign * 2.0 * m) * v1_o[i]
                        if v2[i] is not None:
                            r_m = r_m + float(2 * m * m) * v2[i]
                    table_p[m, part * 5 + i, window] = p_m
                    table_r[m, part * 5 + i, window] = r_m

    def expand(c, start):
        window = pl.ds(start, 8)
        d = [field[i, c, window] for i in range(10)]

        def one(pair, sums):
            alpha = (STEP * 0.05) * forced[0, pair].astype(F32)
            m = forced[1, pair]
            square = alpha * alpha
            q = []
            for i in range(10):
                other = (i + 5) % 10
                turned = alpha * table_r[m, other, window]
                even = table_p[m, i, window] - square * d[i]
                q.append(even - turned if i < 5 else even + turned)
            for i in range(10):
                result[c - 1, pair, i, window] = q[i]
            return (
                sums[0] + (q[1] * q[1] + q[6] * q[6]),
                sums[1] + (q[1] * q[2] + q[6] * q[7]),
                sums[2] + (q[2] * q[2] + q[7] * q[7]),
                sums[3] + (q[3] * q[3] + q[8] * q[8]),
            )

        zero = jnp.zeros((8, LANES), F32)
        sums = lax.fori_loop(0, pairs, one, (zero,) * 4, unroll=2)
        keep = inside(start) * (1.0 / pairs)
        for i in range(4):
            stress[i, c, window] = jnp.where(keep > 0.0, sums[i] * keep, 0.0)

    def out_copy(c):
        lanes = pl.ds(pl.multiple_of((c - 1) * LANES, LANES), LANES)
        return pltpu.make_async_copy(result.at[c - 1, :, :, own], responses.at[:, :, :, lanes], out_sem.at[c - 1])

    def second_stage(c, carry):
        for start in range(6, rows + HALO + 2, 8):
            tables(c, start)
        for start in range(6, rows + HALO + 2, 8):
            expand(c, start)
        out_copy(c).start()
        return carry

    lax.fori_loop(1, blocks + 1, second_stage, 0)

    total = jnp.zeros((8, LANES), F32)
    for c in range(1, blocks + 1):
        ir = inverse_r(c)
        for start in range(HALO, HALO + rows, 8):
            nu = at(field, 15, c, start)

            def laplace(index):
                near = axial(field, index, c, start)
                left, right = radial(field, index, c, start)
                here = at(field, index, c, start)
                second = (16.0 * (near[1] + near[2]) - (near[0] + near[3]) - 30.0 * here) * (1.0 / 12.0)
                return second + (right - 2.0 * here + left)

            def along(index):
                return (1.0 / 12.0) * twelve(axial(stress, index, c, start))

            def across(index):
                left, right = radial(stress, index, c, start)
                return 0.5 * (right - left)

            s1, s2, s3 = [at(stress, i, c, start) for i in (1, 2, 3)]
            first_part = nu * laplace(11) - (along(0) + across(1) + s1 * ir)
            second_part = nu * laplace(12) - (along(1) + across(2) + (s2 - s3) * ir)
            place = (pl.ds(start - HALO, 8), pl.ds((c - 1) * LANES, LANES))
            increment[(0,) + place] = first_part
            increment[(1,) + place] = second_part
            total = total + (first_part * first_part + second_part * second_part)
    squares[...] = jnp.sum(total, axis=0, keepdims=True)
    last = [
        pltpu.make_async_copy(squares, squares_out, end_sem.at[0]),
        pltpu.make_async_copy(increment, increment_out, end_sem.at[1]),
    ]
    for copy in last:
        copy.start()
    for copy in last:
        copy.wait()
    for c in range(1, blocks + 1):
        out_copy(c).wait()


def respond(count, forced, forcing, density, velocity, pressure, visc, cells, halo, halo_cells):
    rows, radial = density.shape
    pairs = forced.shape[1]
    blocks = radial // LANES
    ext = rows + 2 * HALO
    anywhere = pl.BlockSpec(memory_space=pltpu.HBM)
    return pl.pallas_call(
        functools.partial(response_kernel, count, rows, blocks, pairs),
        out_shape=(
            jax.ShapeDtypeStruct((pairs, 10, rows, radial), F32),
            jax.ShapeDtypeStruct((2, rows, radial), F32),
            jax.ShapeDtypeStruct((1, LANES), F32),
        ),
        in_specs=[pl.BlockSpec(memory_space=pltpu.SMEM)] + [anywhere] * 8,
        out_specs=(anywhere, anywhere, anywhere),
        scratch_shapes=[
            pltpu.VMEM((2, rows, radial), F32),
            pltpu.VMEM((1, LANES), F32),
            pltpu.VMEM((16, blocks + 2, ext, LANES), F32),
            pltpu.VMEM((blocks + 2, ext, LANES), jnp.int32),
            pltpu.VMEM((26, blocks + 2, ext, LANES), F32),
            pltpu.VMEM((4, blocks + 2, ext, LANES), F32),
            pltpu.VMEM((WAVES, 10, ext, LANES), F32),
            pltpu.VMEM((WAVES, 10, ext, LANES), F32),
            pltpu.VMEM((blocks, pairs, 10, ext, LANES), F32),
            pltpu.SemaphoreType.DMA((blocks * 10,)),
            pltpu.SemaphoreType.DMA((blocks,)),
            pltpu.SemaphoreType.DMA((2,)),
        ],
        compiler_params=pltpu.CompilerParams(vmem_limit_bytes=67043328),
    )(forced, forcing, density, velocity, pressure, visc, cells, halo, halo_cells)


def normalize_kernel(count, cells, squares, increment, correction, own, held, parts, send, recv, load):
    me = lax.axis_index("axial")
    barrier = pltpu.get_barrier_semaphore()
    others = [lax.rem(me + hop, count) for hop in range(1, count)]
    for other in others:
        pl.semaphore_signal(barrier, inc=1, device_id={"axial": other}, device_id_type=pl.DeviceIdType.MESH)
    loads = [
        pltpu.make_async_copy(squares, own, load.at[0]),
        pltpu.make_async_copy(increment, held, load.at[1]),
    ]
    for copy in loads:
        copy.start()
    pl.semaphore_wait(barrier, count - 1)
    copies = [
        pltpu.make_async_remote_copy(
            src_ref=squares,
            dst_ref=parts.at[hop],
            send_sem=send.at[hop],
            recv_sem=recv.at[hop],
            device_id={"axial": other},
            device_id_type=pl.DeviceIdType.MESH,
        )
        for hop, other in enumerate(others)
    ]
    for copy in copies:
        copy.start()
    for copy in loads:
        copy.wait()
    for copy in copies:
        copy.wait()
    total = own[...]
    for hop in range(count - 1):
        total = total + parts[hop]
    total = jnp.sum(total, axis=1, keepdims=True)
    inverse = 1.0 / jnp.sqrt(total / cells + 1e-06)
    correction[...] = held[...] * inverse


def normalize(count, cells, squares, increment):
    anywhere = pl.BlockSpec(memory_space=pltpu.HBM)
    return pl.pallas_call(
        functools.partial(normalize_kernel, count, cells),
        out_shape=jax.ShapeDtypeStruct(increment.shape, F32),
        in_specs=[anywhere, anywhere],
        out_specs=pl.BlockSpec(memory_space=pltpu.VMEM),
        scratch_shapes=[
            pltpu.VMEM((1, LANES), F32),
            pltpu.VMEM(increment.shape, F32),
            pltpu.VMEM((count - 1, 1, LANES), F32),
            pltpu.SemaphoreType.DMA((count - 1,)),
            pltpu.SemaphoreType.DMA((count - 1,)),
            pltpu.SemaphoreType.DMA((2,)),
        ],
        compiler_params=pltpu.CompilerParams(collective_id=1, has_side_effects=True),
    )(squares, increment)


def shards(count, forced, cells, density, velocity, pressure, visc, forcing):
    rows, radial = density.shape
    pairs = forced.shape[0]
    drive = forcing.reshape(10, rows, radial)
    halo, halo_cells = exchange(count, drive, density, velocity, pressure, visc, cells)
    responses, increment, squares = respond(
        count, forced.T, drive, density, velocity, pressure, visc, cells, halo, halo_cells
    )
    correction = normalize(count, 2 * rows * count * radial, squares, increment)
    return (responses.reshape(pairs, 2, 5, rows, radial), correction)


def solution(mesh):
    placed = (
        P("case", None),
        P(("case", "axial"), None),
        P(("case", "axial"), None),
        P("case", "axial", None),
        P(("case", "axial"), None),
        P(("case", "axial"), None),
        P("case", None, "axial", None),
    )
    return jax.shard_map(
        functools.partial(shards, mesh.shape["axial"]),
        mesh=mesh,
        in_specs=placed,
        out_specs=(P("case", None, None, "axial", None), P("case", "axial", None)),
        check_vma=False,
    )
```

```python
import functools

import jax
import jax.numpy as jnp
from jax import lax
from jax.experimental import pallas as pl
from jax.experimental.pallas import tpu as pltpu
from jax.sharding import PartitionSpec as P

HEAT_RATIO = 1.4
STEP = 0.1
WAVES = 5
HALO = 8
WIDE = 6
NARROW = 4
LANES = 128
F32 = jnp.float32


def exchange_kernel(count, rows, forcing, density, velocity, pressure, visc, cells, halo, halo_cells, send, recv):
    me = lax.axis_index("axial")
    has_low, has_high = me > 0, me < count - 1
    barrier = pltpu.get_barrier_semaphore()

    @pl.when(has_low)
    def _():
        pl.semaphore_signal(barrier, inc=1, device_id={"axial": me - 1}, device_id_type=pl.DeviceIdType.MESH)

    @pl.when(has_high)
    def _():
        pl.semaphore_signal(barrier, inc=1, device_id={"axial": me + 1}, device_id_type=pl.DeviceIdType.MESH)

    @pl.when(has_low & has_high)
    def _():
        pl.semaphore_wait(barrier, 2)

    @pl.when((me == 0) | (me == count - 1))
    def _():
        pl.semaphore_wait(barrier, 1)

    def copies(side):
        target = me + 1 if side == 0 else me - 1

        def cut(reach):
            return pl.ds(rows - reach if side == 0 else 0, reach)

        def to(reach):
            return pl.ds(HALO - reach if side == 0 else 0, reach)

        moves = [
            (forcing.at[:, cut(WIDE), :], halo.at[side, pl.ds(0, 10), to(WIDE)]),
            (velocity.at[:, cut(WIDE), :], halo.at[side, pl.ds(11, 3), to(WIDE)]),
            (density.at[cut(WIDE), :], halo.at[side, 10, to(WIDE)]),
            (pressure.at[cut(WIDE), :], halo.at[side, 14, to(WIDE)]),
            (visc.at[cut(NARROW), :], halo.at[side, 15, to(NARROW)]),
            (cells.at[cut(NARROW), :], halo_cells.at[side, to(NARROW)]),
        ]
        return [
            pltpu.make_async_remote_copy(
                src_ref=src,
                dst_ref=dst,
                send_sem=send.at[side, index],
                recv_sem=recv.at[side, index],
                device_id={"axial": target},
                device_id_type=pl.DeviceIdType.MESH,
            )
            for index, (src, dst) in enumerate(moves)
        ]

    up, down = copies(0), copies(1)

    @pl.when(has_high)
    def _():
        for copy in up:
            copy.start()

    @pl.when(has_low)
    def _():
        for copy in down:
            copy.start()

    @pl.when(has_high)
    def _():
        for copy in up:
            copy.wait_send()
        for copy in down:
            copy.wait_recv()

    @pl.when(has_low)
    def _():
        for copy in down:
            copy.wait_send()
        for copy in up:
            copy.wait_recv()


def exchange(count, forcing, density, velocity, pressure, visc, cells):
    rows, radial = density.shape
    return pl.pallas_call(
        functools.partial(exchange_kernel, count, rows),
        out_shape=(
            jax.ShapeDtypeStruct((2, 16, HALO, radial), F32),
            jax.ShapeDtypeStruct((2, HALO, radial), jnp.int32),
        ),
        in_specs=[pl.BlockSpec(memory_space=pl.ANY)] * 6,
        out_specs=(pl.BlockSpec(memory_space=pl.ANY), pl.BlockSpec(memory_space=pl.ANY)),
        scratch_shapes=[pltpu.SemaphoreType.DMA((2, 6)), pltpu.SemaphoreType.DMA((2, 6))],
        compiler_params=pltpu.CompilerParams(collective_id=0, has_side_effects=True),
    )(forcing, density, velocity, pressure, visc, cells)


def at(ref, index, c, start):
    return ref[index, c, pl.ds(start, 8)]


def axial(ref, index, c, start):
    return [at(ref, index, c, start + offset) for offset in (-2, -1, 1, 2)]


def radial_pair(ref, index, c, start):
    lane = lax.broadcasted_iota(jnp.int32, (8, LANES), 1)
    here = at(ref, index, c, start)
    left = pltpu.roll(jnp.where(lane == LANES - 1, at(ref, index, c - 1, start), here), 1, 1)
    right = pltpu.roll(jnp.where(lane == 0, at(ref, index, c + 1, start), here), LANES - 1, 1)
    return left, right


def twelve(near):
    return (near[0] - near[3]) + 8.0 * (near[2] - near[1])


def inverse_r(c):
    lane = lax.broadcasted_iota(jnp.int32, (8, LANES), 1)
    return 1.0 / (((c - 1) * LANES + lane).astype(F32) + 0.5)


def response_kernel(
    count, rows, blocks, pairs, forced, forcing, density, velocity, pressure, visc, cells, halo, halo_cells,
    responses, stress_out, mean_out,
    field, kind, first, stress, table_p, table_r, result, in_sem, out_sem, end_sem,
):
    me = lax.axis_index("axial")
    all_rows = rows * count
    ext = rows + 2 * HALO
    own = pl.ds(HALO, rows)

    moves = []
    for block in range(blocks):
        lanes = pl.ds(block * LANES, LANES)
        moves += [
            (forcing.at[:, :, lanes], field.at[pl.ds(0, 10), block + 1, own]),
            (velocity.at[:, :, lanes], field.at[pl.ds(11, 3), block + 1, own]),
            (density.at[:, lanes], field.at[10, block + 1, own]),
            (pressure.at[:, lanes], field.at[14, block + 1, own]),
            (visc.at[:, lanes], field.at[15, block + 1, own]),
            (cells.at[:, lanes], kind.at[block + 1, own]),
        ]
        for side, start in ((0, 0), (1, HALO + rows)):
            edge = pl.ds(start, HALO)
            moves += [
                (halo.at[side, :, :, lanes], field.at[:, block + 1, edge]),
                (halo_cells.at[side, :, lanes], kind.at[block + 1, edge]),
            ]
    copies = [pltpu.make_async_copy(src, dst, in_sem.at[i]) for i, (src, dst) in enumerate(moves)]
    for copy in copies:
        copy.start()
    for side in (0, blocks + 1):
        field[:, side] = jnp.zeros((16, ext, LANES), F32)
        first[:, side] = jnp.zeros((26, ext, LANES), F32)
        stress[:, side] = jnp.zeros((4, ext, LANES), F32)
    def settle(block):
        for copy in copies[10 * block : 10 * block + 10]:
            copy.wait()
        c = block + 1

        @pl.when(me == 0)
        def _():
            field[:, c, pl.ds(0, HALO)] = jnp.zeros((16, HALO, LANES), F32)
            kind[c, pl.ds(0, HALO)] = jnp.zeros((HALO, LANES), jnp.int32)

        @pl.when(me == count - 1)
        def _():
            field[:, c, pl.ds(HALO + rows, HALO)] = jnp.zeros((16, HALO, LANES), F32)
            kind[c, pl.ds(HALO + rows, HALO)] = jnp.zeros((HALO, LANES), jnp.int32)

    sub = lax.broadcasted_iota(jnp.int32, (8, LANES), 0)

    def global_row(start):
        return sub + (me * rows + (start - HALO))

    def inside(start):
        row = global_row(start)
        return jnp.where((row >= 0) & (row < all_rows), 1.0, 0.0).astype(F32)

    def scale_drive(c, carry):
        for start in range(0, ext, 8):
            envelope = 0.5 + (global_row(start).astype(F32) + 0.5) / all_rows
            for index in range(10):
                field[index, c, pl.ds(start, 8)] = field[index, c, pl.ds(start, 8)] * envelope
        return carry

    def coefficients(c, start):
        k = {}
        rho, u, v, w, p = [at(field, 10 + i, c, start) for i in range(5)]
        ir = inverse_r(c)
        nu = STEP * at(field, 15, c, start)
        cell = kind[c, pl.ds(start, 8)]
        damp = jnp.where(cell == 1, 2.0, jnp.where(cell == 2, 10.0, 0.0)).astype(F32)
        inv_rho = STEP / jnp.where(rho > 0.0, rho, 1.0)
        for i in range(5):
            left, right = radial_pair(field, 10 + i, c, start)
            k["x", i] = (-STEP / 12.0) * twelve(axial(field, 10 + i, c, start))
            k["r", i] = (-STEP / 2.0) * (right - left)
        swirl = w * ir
        k["r", 3] = k["r", 3] - STEP * swirl
        k["swirl2"] = (2.0 * STEP) * swirl
        k["u12"] = (-STEP / 12.0) * u
        k["v2"] = (-STEP / 2.0) * v
        k["inviscid"] = 1.0 - STEP * damp
        nu12 = nu * (1.0 / 12.0)
        k["viscous"] = k["inviscid"] - nu * 4.5
        k["m2"] = k["u12"] - nu12
        k["m1"] = 16.0 * nu12 - 8.0 * k["u12"]
        k["p1"] = 16.0 * nu12 + 8.0 * k["u12"]
        k["p2"] = -nu12 - k["u12"]
        slope = 0.5 * nu * ir + k["v2"]
        k["left"] = nu - slope
        k["right"] = nu + slope
        k["rho_div"] = -STEP * rho
        k["p_div"] = (-STEP * HEAT_RATIO) * p
        k["px"] = inv_rho * (-1.0 / 12.0)
        k["pr"] = inv_rho * -0.5
        k["ir"] = ir
        k["turn"] = -STEP * swirl
        k["turn_rho"] = -STEP * rho * ir
        k["turn_w"] = -inv_rho * ir
        k["turn_p"] = k["p_div"] * ir
        k["square"] = -nu * ir * ir
        return k

    def base_operator(k, ref, ids, c, start):
        value, ax, rad = {}, {}, {}
        for i in range(5):
            if ids[i] is not None:
                value[i] = at(ref, ids[i], c, start)
                ax[i] = axial(ref, ids[i], c, start)
                rad[i] = radial_pair(ref, ids[i], c, start)
        div = (1.0 / 12.0) * twelve(ax[1]) + 0.5 * (rad[2][1] - rad[2][0]) + value[2] * k["ir"]
        out = []
        for i in range(5):
            if i in (0, 4):
                term = k["rho_div" if i == 0 else "p_div"] * div
                if i in value:
                    term = term + k["inviscid"] * value[i] + k["u12"] * twelve(ax[i]) + k["v2"] * (rad[i][1] - rad[i][0])
            else:
                term = (
                    k["viscous"] * value[i]
                    + (k["m2"] * ax[i][0] + k["m1"] * ax[i][1])
                    + (k["p1"] * ax[i][2] + k["p2"] * ax[i][3])
                    + (k["left"] * rad[i][0] + k["right"] * rad[i][1])
                )
            if i != 3:
                term = term + k["x", i] * value[1]
            term = term + k["r", i] * value[2]
            if i == 1 and 4 in value:
                term = term + k["px"] * twelve(ax[4])
            if i == 2:
                term = term + k["swirl2"] * value[3]
                if 4 in value:
                    term = term + k["pr"] * (rad[4][1] - rad[4][0])
            out.append(term)
        return out

    def turn_operator(k, q):
        out = [None] * 5
        for i in range(5):
            if q[i] is not None:
                out[i] = k["turn"] * q[i]
        for i, source, name in ((0, 3, "turn_rho"), (3, 4, "turn_w"), (4, 3, "turn_p")):
            if q[source] is not None:
                extra = k[name] * q[source]
                out[i] = extra if out[i] is None else out[i] + extra
        return out

    def base(k, ref, ids, c, start):
        out = base_operator(k, ref, ids, c, start)
        return out

    def first_stage(c, carry):
        for start in range(4, rows + 2 * HALO - 4, 8):
            k = coefficients(c, start)
            keep = inside(start)
            for part in range(2):
                d = [at(field, part * 5 + i, c, start) for i in range(5)]
                moved = base(k, field, [part * 5 + i for i in range(5)], c, start)
                turned = turn_operator(k, d)
                for i in range(5):
                    first[part * 5 + i, c, pl.ds(start, 8)] = keep * (moved[i] + STEP * d[i])
                    first[10 + part * 5 + i, c, pl.ds(start, 8)] = keep * turned[i]
                for i in range(1, 4):
                    first[20 + part * 3 + i - 1, c, pl.ds(start, 8)] = keep * (k["square"] * d[i])
        return carry

    for block in range(blocks):
        settle(block)
        scale_drive(block + 1, 0)
        if block > 0:
            first_stage(block, 0)
    mean_copy = pltpu.make_async_copy(field.at[pl.ds(11, 5)], mean_out, end_sem.at[0])
    mean_copy.start()
    first_stage(blocks, 0)

    def tables(c, start):
        k = coefficients(c, start)
        window = pl.ds(start, 8)
        for part in range(2):
            other = 1 - part
            sign = -1.0 if part == 0 else 1.0
            h0 = [part * 5 + i for i in range(5)]
            h0_o = [other * 5 + i for i in range(5)]
            h1 = [10 + part * 5 + i for i in range(5)]
            h1_o = [10 + other * 5 + i for i in range(5)]
            h2 = [None] + [20 + part * 3 + i for i in range(3)] + [None]
            h2_o = [None] + [20 + other * 3 + i for i in range(3)] + [None]

            def values(ids):
                return [None if i is None else at(first, i, c, start) for i in ids]

            d = [at(field, part * 5 + i, c, start) for i in range(5)]
            v0, v0_o, v1, v1_o, v2, v2_o = [values(ids) for ids in (h0, h0_o, h1, h1_o, h2, h2_o)]
            e0 = base(k, first, h0, c, start)
            e1 = base(k, first, h1_o, c, start)
            e2 = base(k, first, h2, c, start)
            t0 = turn_operator(k, v0_o)
            t1 = turn_operator(k, v1)
            t2 = turn_operator(k, v2_o)
            for i in range(5):
                a0 = e0[i] + STEP * d[i]
                a1 = e1[i] + t0[i]
                a2 = e2[i] - t1[i]
                a3 = t2[i]
                a4 = None
                if v2[i] is not None:
                    a2 = a2 + k["square"] * v0[i]
                    a3 = a3 + k["square"] * v1_o[i]
                    a4 = k["square"] * v2[i]
                r0 = 2.0 * v0[i] - STEP * d[i]
                for m in range(WAVES):
                    if m == 0:
                        p_m, r_m = a0, r0
                    else:
                        even = a2 if a4 is None else a2 + float(m * m) * a4
                        odd = a1 + float(m * m) * a3
                        p_m = a0 + float(m * m) * even + (sign * m) * odd
                        r_m = r0 + (sign * 2.0 * m) * v1_o[i]
                        if v2[i] is not None:
                            r_m = r_m + float(2 * m * m) * v2[i]
                    table_p[m, part * 5 + i, window] = p_m
                    table_r[m, part * 5 + i, window] = r_m

    def expand(c, start):
        window = pl.ds(start, 8)
        d = [field[i, c, window] for i in range(10)]

        def one(pair, sums):
            alpha = (STEP * 0.05) * forced[0, pair].astype(F32)
            m = forced[1, pair]
            square = alpha * alpha
            q = []
            for i in range(10):
                other = (i + 5) % 10
                turned = alpha * table_r[m, other, window]
                even = table_p[m, i, window] - square * d[i]
                q.append(even - turned if i < 5 else even + turned)
            for i in range(10):
                result[c - 1, pair, i, window] = q[i]
            return (
                sums[0] + (q[1] * q[1] + q[6] * q[6]),
                sums[1] + (q[1] * q[2] + q[6] * q[7]),
                sums[2] + (q[2] * q[2] + q[7] * q[7]),
                sums[3] + (q[3] * q[3] + q[8] * q[8]),
            )

        zero = jnp.zeros((8, LANES), F32)
        sums = lax.fori_loop(0, pairs, one, (zero,) * 4, unroll=2)
        keep = inside(start) * (1.0 / pairs)
        for i in range(4):
            stress[i, c, window] = jnp.where(keep > 0.0, sums[i] * keep, 0.0)

    def out_copy(c):
        lanes = pl.ds(pl.multiple_of((c - 1) * LANES, LANES), LANES)
        return pltpu.make_async_copy(result.at[c - 1, :, :, own], responses.at[:, :, :, lanes], out_sem.at[c - 1])

    def second_stage(c, carry):
        for start in range(6, rows + HALO + 2, 8):
            tables(c, start)
        for start in range(6, rows + HALO + 2, 8):
            expand(c, start)
        out_copy(c).start()
        return carry

    lax.fori_loop(1, blocks + 1, second_stage, 0)

    stress_copy = pltpu.make_async_copy(stress, stress_out, end_sem.at[1])
    stress_copy.start()
    mean_copy.wait()
    stress_copy.wait()
    for c in range(1, blocks + 1):
        out_copy(c).wait()


def respond(count, forced, forcing, density, velocity, pressure, visc, cells, halo, halo_cells):
    rows, radial = density.shape
    pairs = forced.shape[1]
    blocks = radial // LANES
    ext = rows + 2 * HALO
    anywhere = pl.BlockSpec(memory_space=pltpu.HBM)
    return pl.pallas_call(
        functools.partial(response_kernel, count, rows, blocks, pairs),
        out_shape=(
            jax.ShapeDtypeStruct((pairs, 10, rows, radial), F32),
            jax.ShapeDtypeStruct((4, blocks + 2, ext, LANES), F32),
            jax.ShapeDtypeStruct((5, blocks + 2, ext, LANES), F32),
        ),
        in_specs=[pl.BlockSpec(memory_space=pltpu.SMEM)] + [anywhere] * 8,
        out_specs=(anywhere, anywhere, anywhere),
        scratch_shapes=[
            pltpu.VMEM((16, blocks + 2, ext, LANES), F32),
            pltpu.VMEM((blocks + 2, ext, LANES), jnp.int32),
            pltpu.VMEM((26, blocks + 2, ext, LANES), F32),
            pltpu.VMEM((4, blocks + 2, ext, LANES), F32),
            pltpu.VMEM((WAVES, 10, ext, LANES), F32),
            pltpu.VMEM((WAVES, 10, ext, LANES), F32),
            pltpu.VMEM((blocks, pairs, 10, ext, LANES), F32),
            pltpu.SemaphoreType.DMA((blocks * 10,)),
            pltpu.SemaphoreType.DMA((blocks,)),
            pltpu.SemaphoreType.DMA((2,)),
        ],
        compiler_params=pltpu.CompilerParams(vmem_limit_bytes=67043328),
    )(forced, forcing, density, velocity, pressure, visc, cells, halo, halo_cells)


def normalize_kernel(
    count, rows, blocks, size, stress_in, mean_in, increment_out, inverse,
    stress, field, increment, squares, parts, send, recv, load,
):
    me = lax.axis_index("axial")
    barrier = pltpu.get_barrier_semaphore()
    others = [lax.rem(me + hop, count) for hop in range(1, count)]
    for other in others:
        pl.semaphore_signal(barrier, inc=1, device_id={"axial": other}, device_id_type=pl.DeviceIdType.MESH)
    loads = [
        pltpu.make_async_copy(stress_in, stress, load.at[0]),
        pltpu.make_async_copy(mean_in, field, load.at[1]),
    ]
    for copy in loads:
        copy.start()
    for copy in loads:
        copy.wait()

    def force(c, total):
        ir = inverse_r(c)
        for start in range(HALO, HALO + rows, 8):
            nu = at(field, 4, c, start)

            def laplace(index):
                near = axial(field, index, c, start)
                left, right = radial_pair(field, index, c, start)
                here = at(field, index, c, start)
                second = (16.0 * (near[1] + near[2]) - (near[0] + near[3]) - 30.0 * here) * (1.0 / 12.0)
                return second + (right - 2.0 * here + left)

            def along(index):
                return (1.0 / 12.0) * twelve(axial(stress, index, c, start))

            def across(index):
                left, right = radial_pair(stress, index, c, start)
                return 0.5 * (right - left)

            s1, s2, s3 = [at(stress, i, c, start) for i in (1, 2, 3)]
            first_part = nu * laplace(0) - (along(0) + across(1) + s1 * ir)
            second_part = nu * laplace(1) - (along(1) + across(2) + (s2 - s3) * ir)
            place = (pl.ds(start - HALO, 8), pl.ds(pl.multiple_of((c - 1) * LANES, LANES), LANES))
            increment[(0,) + place] = first_part
            increment[(1,) + place] = second_part
            total = total + (first_part * first_part + second_part * second_part)
        return total

    total = lax.fori_loop(1, blocks + 1, force, jnp.zeros((8, LANES), F32))
    squares[...] = jnp.sum(total, axis=0, keepdims=True)
    pl.semaphore_wait(barrier, count - 1)
    copies = [
        pltpu.make_async_remote_copy(
            src_ref=squares,
            dst_ref=parts.at[hop],
            send_sem=send.at[hop],
            recv_sem=recv.at[hop],
            device_id={"axial": other},
            device_id_type=pl.DeviceIdType.MESH,
        )
        for hop, other in enumerate(others)
    ]
    for copy in copies:
        copy.start()
    keep = pltpu.make_async_copy(increment, increment_out, load.at[2])
    keep.start()
    for copy in copies:
        copy.wait()
    total = squares[...]
    for hop in range(count - 1):
        total = total + parts[hop]
    total = jnp.sum(total, axis=1, keepdims=True)
    inverse[...] = jnp.broadcast_to(1.0 / jnp.sqrt(total / size + 1e-06), inverse.shape)
    keep.wait()


def normalize(count, rows, radial, stress, mean):
    anywhere = pl.BlockSpec(memory_space=pltpu.HBM)
    increment = (2, rows, radial)
    return pl.pallas_call(
        functools.partial(normalize_kernel, count, rows, radial // LANES, 2 * rows * count * radial),
        out_shape=(jax.ShapeDtypeStruct(increment, F32), jax.ShapeDtypeStruct((1, radial), F32)),
        in_specs=[anywhere, anywhere],
        out_specs=(anywhere, pl.BlockSpec(memory_space=pltpu.VMEM)),
        scratch_shapes=[
            pltpu.VMEM(stress.shape, F32),
            pltpu.VMEM(mean.shape, F32),
            pltpu.VMEM(increment, F32),
            pltpu.VMEM((1, LANES), F32),
            pltpu.VMEM((count - 1, 1, LANES), F32),
            pltpu.SemaphoreType.DMA((count - 1,)),
            pltpu.SemaphoreType.DMA((count - 1,)),
            pltpu.SemaphoreType.DMA((3,)),
        ],
        compiler_params=pltpu.CompilerParams(collective_id=1, has_side_effects=True),
    )(stress, mean)


def shards(count, forced, cells, density, velocity, pressure, visc, forcing):
    rows, radial = density.shape
    pairs = forced.shape[0]
    drive = forcing.reshape(10, rows, radial)
    halo, halo_cells = exchange(count, drive, density, velocity, pressure, visc, cells)
    responses, stress, mean = respond(
        count, forced.T, drive, density, velocity, pressure, visc, cells, halo, halo_cells
    )
    increment, inverse = normalize(count, rows, radial, stress, mean)
    return (responses.reshape(pairs, 2, 5, rows, radial), increment * inverse[None])


def solution(mesh):
    placed = (
        P("case", None),
        P(("case", "axial"), None),
        P(("case", "axial"), None),
        P("case", "axial", None),
        P(("case", "axial"), None),
        P(("case", "axial"), None),
        P("case", None, "axial", None),
    )
    return jax.shard_map(
        functools.partial(shards, mesh.shape["axial"]),
        mesh=mesh,
        in_specs=placed,
        out_specs=(P("case", None, None, "axial", None), P("case", "axial", None)),
        check_vma=False,
    )
```
